32 devices in a mesh: tm: 4 (over y, x), space: 8 (over z, core).
Axes of the slice: x: 2, y: 2, z: 4, core: 2. Of those that a mesh axis runs over, the one named last changes fastest.
Arguments:
- image: float32 [16, 256, 512], P('space', None, 'tm'), may hold values from -6 to 6
- inv_var: float32 [16, 256, 512], P('space', None, 'tm'), may hold values from 0.25 to 4
- psf: float32 [15, 15], replicated, may hold values from 0.001 to 1
- shifts: int32 [16, 16, 2], replicated, may hold values from -16 to 16, as said below
Outputs:
- best: float32 [256, 512], P('space', 'tm')
- score: float32 [256, 512], P('space', 'tm')
The draws below stay inside these ranges and needn't reach their ends.
Inputs may be any that keep to these rules, and one draw needn't show every extreme that they name: shifts[v, e, k] = floor(u[v, k] * e / 15) for integer velocities u[v, k] between -16 and 16; u[0] is +16 and u[1] is -16 in both components, so epoch e shifts by at most ceil(16 * e / 15).
All inputs are finite; a program needn't handle non-finite values.
Results may differ from the reference program's by a relative error of at most 0.0048.
Values may be sent and summed in bfloat16 or wider, within the bound.
No kernel may reach another device: no remote copies, remote signals or barrier semaphores. Data moves between devices by JAX's collectives and lax.ppermute only.
A program may use at most 64 MiB of HBM per device.

```python
import math
import jax
import jax.numpy as jnp
from jax import lax

VELS = 16
RADIUS = 7
MAXSHIFT = 16
EPOCHS = 16
WIDTH = 256
HEIGHT = 512


def draw_shifts(key, part):
    speeds = jax.random.randint(key, (VELS, 2), -MAXSHIFT, MAXSHIFT + 1, jnp.int32)
    speeds = speeds.at[0, :].set(MAXSHIFT)
    speeds = speeds.at[1, :].set(-MAXSHIFT)
    epoch_pos = jnp.arange(EPOCHS, dtype=jnp.int32)
    return speeds[:, None, :] * epoch_pos[None, :, None] // (EPOCHS - 1)


def levels(key, dims, cuts, smallest, top_value):
    def one(position, shards_of):
        steps = jax.random.uniform(jax.random.fold_in(jax.random.fold_in(key, 6), position), (shards_of,), jnp.float32, smallest / len(cuts), top_value / len(cuts))
        return jnp.repeat(jnp.exp(steps), dims[position] // shards_of).reshape((-1,) + (1,) * (len(dims) - position - 1))

    loudness = one(*cuts[0])
    for cut in cuts[1:]:
        loudness = loudness * one(*cut)
    return loudness


def normal_values(stream_key, extent, deviation, limit, cuts=(), kind=jnp.bfloat16):
    gain = levels(stream_key, extent, cuts, -0.22, 0.18) if cuts else 1.0
    entries = jax.random.normal(stream_key, extent, jnp.float32) * deviation * gain
    return jnp.minimum(jnp.maximum(entries, -limit), limit).astype(kind)


def setup_inputs(seed: int = 0) -> dict:
    splits = jax.random.split(jax.random.key(seed), 5)
    return {
        "image": normal_values(splits[0], (EPOCHS, WIDTH, HEIGHT), 1.0, 6.0, ((0, 8), (2, 4)), jnp.float32),
        "inv_var": jnp.clip(jnp.exp(math.log(4.0) - 2.7725887 * jax.random.uniform(splits[1], (EPOCHS, WIDTH, HEIGHT), jnp.float32) ** levels(splits[1], (EPOCHS, WIDTH, HEIGHT), ((0, 8), (2, 4)), -0.2, 0.2)), 0.25, 4.0),
        "psf": jnp.clip(jnp.exp(jax.random.uniform(splits[2], (2 * RADIUS + 1, 2 * RADIUS + 1), jnp.float32, math.log(0.001), math.log(1.0))), 0.001, 1.0),
        "shifts": draw_shifts(jax.random.fold_in(splits[4], 71), 0),
    }


def correlate(frames, kern):
    out = lax.conv_general_dilated(frames[:, None], kern[None, None], (1, 1), ((RADIUS, RADIUS), (RADIUS, RADIUS)), preferred_element_type=jnp.float32)
    return out[:, 0]

def likelihood(shifted_psi, shifted_phi, axis):
    psi_part = shifted_psi.astype(jnp.float32)
    phi_part = shifted_phi.astype(jnp.float32)
    signal = jnp.abs(psi_part) / jnp.sqrt(jnp.maximum(phi_part, 0.001))
    weight = jax.nn.sigmoid(2.0 * (2.0 - signal))
    upper = lax.optimization_barrier(jnp.sum(weight * psi_part, axis=axis))
    lower = lax.optimization_barrier(jnp.sum(weight * phi_part, axis=axis))
    return upper / jnp.sqrt(jnp.maximum(lower, 0.02))

def reference(image, inv_var, psf, shifts):
    normed = psf / jnp.sum(psf)
    kern = normed.astype(jnp.bfloat16)
    kern_sq = (normed * normed).astype(jnp.bfloat16)
    weighted = (image * inv_var).astype(jnp.bfloat16)
    variance = inv_var.astype(jnp.bfloat16)
    psi = correlate(weighted, kern).astype(jnp.bfloat16)
    phi = correlate(variance, kern_sq).astype(jnp.bfloat16)
    both = jnp.stack([psi, phi], 1)
    padded = jnp.pad(both, ((0, 0), (0, 0), (MAXSHIFT, MAXSHIFT), (MAXSHIFT, MAXSHIFT)))
    zero = jnp.zeros((), jnp.int32)

    def cut(frame, shift):
        return lax.dynamic_slice(frame, (zero, (MAXSHIFT + shift[0]).astype(jnp.int32), (MAXSHIFT + shift[1]).astype(jnp.int32)), (2, WIDTH, HEIGHT))

    def visit(carry, shift_v):
        top, total = carry
        pieces = jax.vmap(cut)(padded, shift_v)
        like = likelihood(pieces[:, 0], pieces[:, 1], 0)
        return ((jnp.maximum(top, like), total + jnp.exp(like)), None)
    start = (jnp.full((WIDTH, HEIGHT), -jnp.inf, jnp.float32), jnp.zeros((WIDTH, HEIGHT), jnp.float32))
    (top, total), unused = lax.scan(visit, start, shifts)
    return (top, jnp.log(total / VELS))
```

```python
import functools

import jax
import jax.numpy as jnp
from jax import lax
from jax.experimental import pallas as pl
from jax.experimental.pallas import tpu as pltpu
from jax.sharding import PartitionSpec as P

RADIUS = 7
TAPS = 2 * RADIUS + 1
MAXSHIFT = 16
LANES = 128
HALO = 24
BLOCK = 256
F32 = jnp.float32
BF16 = jnp.bfloat16
VMEM = pl.BlockSpec(memory_space=pltpu.VMEM)
SMEM = pl.BlockSpec(memory_space=pltpu.SMEM)
PARAMS = pltpu.CompilerParams(vmem_limit_bytes=48 * 1024 * 1024)


def prepare_kernel(image_ref, inv_var_ref, main_ref, first_ref, last_ref):
    epochs, _, rows = image_ref.shape
    for ep in range(epochs):
        inv_var = inv_var_ref[ep]
        for plane, values in ((0, image_ref[ep] * inv_var), (1, inv_var)):
            turned = values.T.astype(BF16)
            main_ref[plane, ep] = turned
            first_ref[plane, ep] = turned[:HALO]
            last_ref[plane, ep] = turned[rows - HALO :]


def prepare(image, inv_var):
    epochs, width, rows = image.shape
    halo = jax.ShapeDtypeStruct((2, epochs, HALO, width), BF16)
    return pl.pallas_call(
        prepare_kernel,
        out_shape=(jax.ShapeDtypeStruct((2, epochs, rows, width), BF16), halo, halo),
        in_specs=[VMEM] * 2,
        out_specs=[VMEM] * 3,
        compiler_params=PARAMS,
        name="prepare",
    )(image, inv_var)


def band_kernel(psf_ref, band_ref, corner_ref):
    psf = psf_ref[...]
    normed = psf / jnp.sum(psf)
    flip = (
        lax.broadcasted_iota(jnp.int32, (TAPS, LANES), 0)
        + lax.broadcasted_iota(jnp.int32, (TAPS, LANES), 1)
        == TAPS - 1
    ).astype(BF16)
    size = (LANES, LANES)
    ahead = lax.broadcasted_iota(jnp.int32, size, 1) - lax.broadcasted_iota(jnp.int32, size, 0)
    near = jnp.abs(ahead) <= LANES // 2
    below = ahead > LANES // 2
    above = ahead < -(LANES // 2)
    for plane, kern in ((0, normed.astype(BF16)), (1, (normed * normed).astype(BF16))):
        taps = lax.dot_general(kern, flip, (((0,), (0,)), ((), ())), preferred_element_type=F32)
        for j in range(TAPS):
            spread = jnp.broadcast_to(taps[j : j + 1, :], size)
            ring = pltpu.roll(spread, LANES - RADIUS, 1, stride=1, stride_axis=0)
            diagonal = jnp.where(near, ring, 0.0).astype(BF16)
            at = j * BLOCK
            band_ref[plane, at : at + LANES, :LANES] = diagonal
            band_ref[plane, at + LANES : at + BLOCK, LANES:] = diagonal
            from_left = jnp.where(above, ring, 0.0).astype(BF16)
            from_right = jnp.where(below, ring, 0.0).astype(BF16)
            band_ref[plane, at : at + LANES, LANES:] = from_left
            band_ref[plane, at + LANES : at + BLOCK, :LANES] = from_right
            corner_ref[plane, 0, j * LANES : (j + 1) * LANES] = from_left
            corner_ref[plane, 1, j * LANES : (j + 1) * LANES] = from_right


def band_matrices(psf):
    return pl.pallas_call(
        band_kernel,
        out_shape=(
            jax.ShapeDtypeStruct((2, TAPS * BLOCK, BLOCK), BF16),
            jax.ShapeDtypeStruct((2, 2, TAPS * LANES, LANES), BF16),
        ),
        in_specs=[VMEM],
        out_specs=[VMEM] * 2,
        compiler_params=PARAMS,
        name="band",
    )(psf)


def filter_kernel(chips, where_ref, main_ref, before_ref, after_ref, band_ref, corner_ref, *refs):
    outs, (tall, lhs, corner_lhs, turned, wide) = refs[:chips], refs[chips:]
    _, epochs, rows, width = main_ref.shape
    out_rows = rows + 2 * MAXSHIFT
    for plane in range(2):
        for ep in range(epochs):
            tall[plane, ep, :HALO] = before_ref[plane, ep]
            tall[plane, ep, HALO : HALO + rows] = main_ref[plane, ep]
            tall[plane, ep, HALO + rows :] = after_ref[plane, ep]
    chip, row_block, height = where_ref[0], where_ref[1], where_ref[2]
    row = row_block * rows - MAXSHIFT + lax.broadcasted_iota(jnp.int32, (out_rows, BLOCK), 0)
    inside = (row >= 0) & (row < height)
    skip = HALO - MAXSHIFT - RADIUS
    blocks = width // BLOCK
    for block in range(blocks):
        at = block * BLOCK
        filtered = []
        for plane in range(2):
            for ep in range(epochs):
                for j in range(TAPS):
                    lhs[ep * out_rows : (ep + 1) * out_rows, j * BLOCK : (j + 1) * BLOCK] = tall[
                        plane, ep, skip + j : skip + j + out_rows, at : at + BLOCK
                    ]
            total = jnp.dot(lhs[...], band_ref[plane], preferred_element_type=F32)
            low, high = total[:, :LANES], total[:, LANES:]
            for side, source in ((0, at - LANES), (1, at + BLOCK)):
                if source < 0 or source >= width:
                    continue
                for ep in range(epochs):
                    for j in range(TAPS):
                        corner_lhs[ep * out_rows : (ep + 1) * out_rows, j * LANES : (j + 1) * LANES] = tall[
                            plane, ep, skip + j : skip + j + out_rows, source : source + LANES
                        ]
                more = jnp.dot(corner_lhs[...], corner_ref[plane, side], preferred_element_type=F32)
                low, high = (low + more, high) if side == 0 else (low, high + more)
            total = jnp.concatenate([low, high], axis=1)
            parts = []
            for ep in range(epochs):
                part = total[ep * out_rows : (ep + 1) * out_rows]
                parts.append(jnp.where(inside, part.astype(BF16).astype(F32), 0.0))
            filtered.append(parts)
        for ep in range(epochs):
            psi, phi = filtered[0][ep], filtered[1][ep]
            signal = jnp.abs(psi) * lax.rsqrt(jnp.maximum(phi, 0.001))
            weight = 1.0 / (1.0 + jnp.exp(2.0 * signal - 4.0))
            for plane, values in ((0, weight * psi), (1, weight * phi)):
                slot = 2 * ep + plane
                turn = (MAXSHIFT * 2 * slot) % rows
                base = slot * LANES
                turned[base + turn : base + rows, :] = values[: rows - turn]
                if turn:
                    turned[base : base + turn, :] = values[rows - turn : rows]
                extra = 2 * epochs * LANES + slot * 2 * MAXSHIFT
                turned[extra : extra + 2 * MAXSHIFT, :] = values[rows:]
        for part in range(2 * epochs + 1):
            lanes = slice(part * LANES, (part + 1) * LANES)
            wide[MAXSHIFT + at : MAXSHIFT + at + BLOCK, lanes] = turned[lanes, :].T.astype(BF16)
    edge = jnp.zeros((MAXSHIFT, wide.shape[1]), BF16)
    wide[:MAXSHIFT] = edge
    wide[MAXSHIFT + width :] = edge
    span = width // chips
    for k in range(chips):
        other = jnp.bitwise_xor(chip, k)
        start = pl.multiple_of(other * span, span)
        outs[k][...] = wide[pl.ds(start, span + 2 * MAXSHIFT), :]


def filter_epochs(where, main, before, after, band, corner, chips):
    _, epochs, rows, width = main.shape
    out_rows = rows + 2 * MAXSHIFT
    lanes = (2 * epochs + 1) * LANES
    piece = jax.ShapeDtypeStruct((width // chips + 2 * MAXSHIFT, lanes), BF16)
    return pl.pallas_call(
        functools.partial(filter_kernel, chips),
        out_shape=(piece,) * chips,
        in_specs=[SMEM] + [VMEM] * 5,
        out_specs=[VMEM] * chips,
        scratch_shapes=[
            pltpu.VMEM((2, epochs, rows + 2 * HALO, width), BF16),
            pltpu.VMEM((epochs * out_rows, TAPS * BLOCK), BF16),
            pltpu.VMEM((epochs * out_rows, TAPS * LANES), BF16),
            pltpu.VMEM((lanes, BLOCK), F32),
            pltpu.VMEM((width + 2 * MAXSHIFT, lanes), BF16),
        ],
        compiler_params=PARAMS,
        name="filter",
    )(where, main, before, after, band, corner)


def stack_kernel(chips, vels, where_ref, shifts_ref, *refs):
    pieces, (best_ref, score_ref), (frames,) = refs[: 2 * chips], refs[2 * chips : -1], refs[-1:]
    chip, core = where_ref[0], where_ref[3]
    cols, rows = best_ref.shape
    window = cols + 2 * MAXSHIFT
    parts = pieces[0].shape[1] // LANES
    epochs = (parts - 1) // 2
    start = pl.multiple_of(core * cols, cols)
    for slot in range(2 * chips):
        for part in range(parts):
            base = (slot * parts + part) * window
            frames[base : base + window] = pieces[slot][
                pl.ds(start, window), part * LANES : (part + 1) * LANES
            ].astype(F32)
    lane = lax.broadcasted_iota(jnp.int32, (cols, LANES), 1)

    def add_slot(slot, v, upper, lower):
        if isinstance(slot, int):
            k, flip = slot // 2, slot % 2
        else:
            k, flip = lax.div(slot, 2), lax.rem(slot, 2)
        owner = 2 * jnp.bitwise_xor(chip, k) + jnp.bitwise_xor(core, flip)
        for ep in range(epochs):
            epoch = owner * epochs + ep
            right = MAXSHIFT + shifts_ref[2 * v, epoch]
            down = MAXSHIFT + shifts_ref[2 * v + 1, epoch]
            base = slot * (parts * window) + right
            extra = frames[pl.ds(base + 2 * epochs * window, cols), :]
            sums = []
            for plane, total in ((0, upper), (1, lower)):
                part = 2 * ep + plane
                turn = 2 * MAXSHIFT * part
                place = lane if turn == 0 else lax.rem(lane + (LANES - turn), LANES)
                held = frames[pl.ds(base + part * window, cols), :]
                merged = jnp.where(place < down, extra, held)
                sums.append(total + pltpu.roll(merged, lax.rem(2 * LANES - turn - down, LANES), 1))
            upper, lower = sums
        return upper, lower

    def visit(v, carry):
        top, total = carry
        upper = jnp.zeros((cols, LANES), F32)
        lower = jnp.zeros((cols, LANES), F32)
        group = 8
        if 2 * chips <= group:
            for slot in range(2 * chips):
                upper, lower = add_slot(slot, v, upper, lower)
        else:
            def some(g, sums):
                for s in range(group):
                    sums = add_slot(g * group + s, v, *sums)
                return sums

            upper, lower = lax.fori_loop(0, 2 * chips // group, some, (upper, lower))
        like = upper * lax.rsqrt(jnp.maximum(lower, 0.02))
        return jnp.maximum(top, like), total + jnp.exp(like)

    top = jnp.full((cols, LANES), -jnp.inf, F32)
    top, total = lax.fori_loop(0, vels, visit, (top, jnp.zeros((cols, LANES), F32)))
    best_ref[...] = top
    score_ref[...] = jnp.log(total / vels)


def stack_epochs(where, shifts, pieces, cols, rows):
    vels = shifts.shape[0] // 2
    chips = len(pieces) // 2
    parts = pieces[0].shape[1] // LANES
    out = jax.ShapeDtypeStruct((cols, rows), F32)
    return pl.pallas_call(
        functools.partial(stack_kernel, chips, vels),
        out_shape=(out, out),
        in_specs=[SMEM] * 2 + [VMEM] * (2 * chips),
        out_specs=[VMEM] * 2,
        scratch_shapes=[pltpu.VMEM((2 * chips * parts * (cols + 2 * MAXSHIFT), LANES), F32)],
        compiler_params=PARAMS,
        name="stack",
    )(where, shifts, *pieces)


def on_device(image, inv_var, psf, shifts):
    epochs, width, rows = image.shape
    devices = lax.axis_size("space")
    row_blocks = lax.axis_size("tm")
    chips = devices // 2
    place, row_block = lax.axis_index("space"), lax.axis_index("tm")
    where = jnp.stack([place // 2, row_block, rows * row_blocks, place % 2]).astype(jnp.int32)
    table = jnp.transpose(shifts, (0, 2, 1)).reshape(2 * shifts.shape[0], shifts.shape[1])

    main, first, last = prepare(image, inv_var)
    up = [(i, i + 1) for i in range(row_blocks - 1)]
    down = [(j, i) for i, j in up]
    before = lax.ppermute(last, "tm", up)
    after = lax.ppermute(first, "tm", down)
    band, corner = band_matrices(psf)
    sent = filter_epochs(where, main, before, after, band, corner, chips)

    swap = [(i, i ^ 1) for i in range(devices)]
    got = {0: sent[0]}
    for k in reversed(range(1, chips)):
        pairs = [(2 * i + c, 2 * (i ^ k) + c) for i in range(chips) for c in range(2)]
        got[k] = lax.ppermute(sent[k], "space", pairs)
    pieces = []
    for k in range(chips):
        pieces += [got[k], lax.ppermute(got[k], "space", swap)]
    return stack_epochs(where, table, pieces, width // devices, rows)


def solution(mesh):
    in_specs = (P("space", None, "tm"), P("space", None, "tm"), P(), P())
    out_specs = (P("space", "tm"), P("space", "tm"))
    return jax.shard_map(
        on_device, mesh=mesh, in_specs=in_specs, out_specs=out_specs, check_vma=False
    )
```

```python
import functools

import jax
import jax.numpy as jnp
from jax import lax
from jax.experimental import pallas as pl
from jax.experimental.pallas import tpu as pltpu
from jax.sharding import PartitionSpec as P

RADIUS = 7
TAPS = 2 * RADIUS + 1
MAXSHIFT = 16
LANES = 128
HALO = 24
BLOCK = 256
F32 = jnp.float32
BF16 = jnp.bfloat16
VMEM = pl.BlockSpec(memory_space=pltpu.VMEM)
SMEM = pl.BlockSpec(memory_space=pltpu.SMEM)
PARAMS = pltpu.CompilerParams(vmem_limit_bytes=24 * 1024 * 1024)


def prepare_kernel(weighted_ref, variance_ref, main_ref, even_ref, odd_ref):
    epochs, _, rows = weighted_ref.shape
    even = lax.rem(lax.axis_index("tm"), 2) == 0
    for ep in range(epochs):
        for plane, ref in ((0, weighted_ref), (1, variance_ref)):
            turned = ref[ep].astype(F32).T
            main_ref[plane, ep] = turned.astype(BF16)
            first, last = turned[:HALO], turned[rows - HALO :]
            even_ref[plane, ep] = jnp.where(even, last, first).astype(BF16)
            odd_ref[plane, ep] = jnp.where(even, first, last).astype(BF16)


def prepare(image, inv_var):
    epochs, width, rows = image.shape
    halo = jax.ShapeDtypeStruct((2, epochs, HALO, width), BF16)
    return pl.pallas_call(
        prepare_kernel,
        out_shape=(jax.ShapeDtypeStruct((2, epochs, rows, width), BF16), halo, halo),
        in_specs=[VMEM] * 2,
        out_specs=[VMEM] * 3,
        compiler_params=PARAMS,
        name="prepare",
    )((image * inv_var).astype(BF16), inv_var.astype(BF16))


def band_kernel(psf_ref, band_ref, *corner_refs):
    psf = psf_ref[...]
    normed = psf / jnp.sum(psf)
    flip = (
        lax.broadcasted_iota(jnp.int32, (TAPS, LANES), 0)
        + lax.broadcasted_iota(jnp.int32, (TAPS, LANES), 1)
        == TAPS - 1
    ).astype(BF16)
    size = (LANES, LANES)
    ahead = lax.broadcasted_iota(jnp.int32, size, 1) - lax.broadcasted_iota(jnp.int32, size, 0)
    near = jnp.abs(ahead) <= LANES // 2
    below = ahead > LANES // 2
    above = ahead < -(LANES // 2)
    for plane, kern in ((0, normed.astype(BF16)), (1, (normed * normed).astype(BF16))):
        taps = lax.dot_general(kern, flip, (((0,), (0,)), ((), ())), preferred_element_type=F32)
        for j in range(TAPS):
            spread = jnp.broadcast_to(taps[j : j + 1, :], size)
            ring = pltpu.roll(spread, LANES - RADIUS, 1, stride=1, stride_axis=0)
            diagonal = jnp.where(near, ring, 0.0).astype(BF16)
            at = j * BLOCK
            band_ref[plane, at : at + LANES, :LANES] = diagonal
            band_ref[plane, at + LANES : at + BLOCK, LANES:] = diagonal
            from_left = jnp.where(above, ring, 0.0).astype(BF16)
            from_right = jnp.where(below, ring, 0.0).astype(BF16)
            band_ref[plane, at : at + LANES, LANES:] = from_left
            band_ref[plane, at + LANES : at + BLOCK, :LANES] = from_right
            for corner_ref in corner_refs:
                corner_ref[plane, 0, j * LANES : (j + 1) * LANES] = from_left
                corner_ref[plane, 1, j * LANES : (j + 1) * LANES] = from_right


def band_matrices(psf, blocks):
    shapes = [jax.ShapeDtypeStruct((2, TAPS * BLOCK, BLOCK), BF16)]
    if blocks > 1:
        shapes.append(jax.ShapeDtypeStruct((2, 2, TAPS * LANES, LANES), BF16))
    return pl.pallas_call(
        band_kernel,
        out_shape=shapes,
        in_specs=[VMEM],
        out_specs=[VMEM] * len(shapes),
        compiler_params=PARAMS,
        name="band",
    )(psf)


def filter_kernel(chips, where_ref, main_ref, even_ref, odd_ref, band_ref, *refs):
    blocks = main_ref.shape[3] // BLOCK
    if blocks > 1:
        corner_ref, refs = refs[0], refs[1:]
    outs, (tall, lhs, corner_lhs, turned, wide) = refs[:chips], refs[chips:]
    _, epochs, rows, width = main_ref.shape
    out_rows = rows + 2 * MAXSHIFT
    chip, row_block, height = where_ref[0], where_ref[1], where_ref[2]
    even = lax.rem(row_block, 2) == 0
    for plane in range(2):
        for ep in range(epochs):
            tall[plane, ep, HALO : HALO + rows] = main_ref[plane, ep]
    for is_even, before_ref, after_ref in ((True, odd_ref, even_ref), (False, even_ref, odd_ref)):

        @pl.when(even == is_even)
        def _():
            for plane in range(2):
                for ep in range(epochs):
                    tall[plane, ep, :HALO] = before_ref[plane, ep]
                    tall[plane, ep, HALO + rows :] = after_ref[plane, ep]

    row = row_block * rows - MAXSHIFT + lax.broadcasted_iota(jnp.int32, (out_rows, BLOCK), 0)
    inside = (row >= 0) & (row < height)
    skip = HALO - MAXSHIFT - RADIUS
    for block in range(blocks):
        at = block * BLOCK
        filtered = []
        for plane in range(2):
            for ep in range(epochs):
                for j in range(TAPS):
                    lhs[ep * out_rows : (ep + 1) * out_rows, j * BLOCK : (j + 1) * BLOCK] = tall[
                        plane, ep, skip + j : skip + j + out_rows, at : at + BLOCK
                    ]
            total = jnp.dot(lhs[...], band_ref[plane], preferred_element_type=F32)
            low, high = total[:, :LANES], total[:, LANES:]
            for side, source in ((0, at - LANES), (1, at + BLOCK)):
                if source < 0 or source >= width:
                    continue
                for ep in range(epochs):
                    for j in range(TAPS):
                        corner_lhs[ep * out_rows : (ep + 1) * out_rows, j * LANES : (j + 1) * LANES] = tall[
                            plane, ep, skip + j : skip + j + out_rows, source : source + LANES
                        ]
                more = jnp.dot(corner_lhs[...], corner_ref[plane, side], preferred_element_type=F32)
                low, high = (low + more, high) if side == 0 else (low, high + more)
            total = jnp.concatenate([low, high], axis=1)
            parts = []
            for ep in range(epochs):
                part = total[ep * out_rows : (ep + 1) * out_rows]
                parts.append(jnp.where(inside, part.astype(BF16).astype(F32), 0.0))
            filtered.append(parts)
        for ep in range(epochs):
            psi, phi = filtered[0][ep], filtered[1][ep]
            signal = jnp.abs(psi) * lax.rsqrt(jnp.maximum(phi, 0.001))
            weight = 1.0 / (1.0 + jnp.exp(2.0 * signal - 4.0))
            for plane, values in ((0, weight * psi), (1, weight * phi)):
                slot = 2 * ep + plane
                turn = (MAXSHIFT * 2 * slot) % rows
                base = slot * LANES
                turned[base + turn : base + rows, :] = values[: rows - turn]
                if turn:
                    turned[base : base + turn, :] = values[rows - turn : rows]
                extra = 2 * epochs * LANES + slot * 2 * MAXSHIFT
                turned[extra : extra + 2 * MAXSHIFT, :] = values[rows:]
        for part in range(2 * epochs + 1):
            lanes = slice(part * LANES, (part + 1) * LANES)
            wide[MAXSHIFT + at : MAXSHIFT + at + BLOCK, lanes] = turned[lanes, :].T.astype(BF16)
    edge = jnp.zeros((MAXSHIFT, wide.shape[1]), BF16)
    wide[:MAXSHIFT] = edge
    wide[MAXSHIFT + width :] = edge
    span = width // chips
    for k in range(chips):
        other = jnp.bitwise_xor(chip, k)
        start = pl.multiple_of(other * span, span)
        outs[k][...] = wide[pl.ds(start, span + 2 * MAXSHIFT), :]


def filter_epochs(where, main, even, odd, bands, chips):
    _, epochs, rows, width = main.shape
    out_rows = rows + 2 * MAXSHIFT
    lanes = (2 * epochs + 1) * LANES
    piece = jax.ShapeDtypeStruct((width // chips + 2 * MAXSHIFT, lanes), BF16)
    return pl.pallas_call(
        functools.partial(filter_kernel, chips),
        out_shape=(piece,) * chips,
        in_specs=[SMEM] + [VMEM] * (3 + len(bands)),
        out_specs=[VMEM] * chips,
        scratch_shapes=[
            pltpu.VMEM((2, epochs, rows + 2 * HALO, width), BF16),
            pltpu.VMEM((epochs * out_rows, TAPS * BLOCK), BF16),
            pltpu.VMEM((epochs * out_rows, TAPS * LANES), BF16),
            pltpu.VMEM((lanes, BLOCK), F32),
            pltpu.VMEM((width + 2 * MAXSHIFT, lanes), BF16),
        ],
        compiler_params=PARAMS,
        name="filter",
    )(where, main, even, odd, *bands)


def stack_kernel(chips, vels, where_ref, shifts_ref, *refs):
    pieces, (best_ref, score_ref), (frames,) = refs[: 2 * chips], refs[2 * chips : -1], refs[-1:]
    chip, core = where_ref[0], where_ref[3]
    cols, rows = best_ref.shape
    window = cols + 2 * MAXSHIFT
    parts = pieces[0].shape[1] // LANES
    epochs = (parts - 1) // 2
    start = pl.multiple_of(core * cols, cols)
    for slot in range(2 * chips):
        for part in range(parts):
            base = (slot * parts + part) * window
            frames[base : base + window] = pieces[slot][
                pl.ds(start, window), part * LANES : (part + 1) * LANES
            ].astype(F32)
    lane = lax.broadcasted_iota(jnp.int32, (cols, LANES), 1)

    def add_slot(slot, v, upper, lower):
        if isinstance(slot, int):
            k, flip = slot // 2, slot % 2
        else:
            k, flip = lax.div(slot, 2), lax.rem(slot, 2)
        owner = 2 * jnp.bitwise_xor(chip, k) + jnp.bitwise_xor(core, flip)
        for ep in range(epochs):
            epoch = owner * epochs + ep
            right = MAXSHIFT + shifts_ref[2 * v, epoch]
            down = MAXSHIFT + shifts_ref[2 * v + 1, epoch]
            base = slot * (parts * window) + right
            extra = frames[pl.ds(base + 2 * epochs * window, cols), :]
            sums = []
            for plane, total in ((0, upper), (1, lower)):
                part = 2 * ep + plane
                turn = 2 * MAXSHIFT * part
                place = lane if turn == 0 else lax.rem(lane + (LANES - turn), LANES)
                held = frames[pl.ds(base + part * window, cols), :]
                merged = jnp.where(place < down, extra, held)
                sums.append(total + pltpu.roll(merged, lax.rem(2 * LANES - turn - down, LANES), 1))
            upper, lower = sums
        return upper, lower

    def visit(v, carry):
        top, total = carry
        upper = jnp.zeros((cols, LANES), F32)
        lower = jnp.zeros((cols, LANES), F32)
        group = 8
        if 2 * chips <= group:
            for slot in range(2 * chips):
                upper, lower = add_slot(slot, v, upper, lower)
        else:
            def some(g, sums):
                for s in range(group):
                    sums = add_slot(g * group + s, v, *sums)
                return sums

            upper, lower = lax.fori_loop(0, 2 * chips // group, some, (upper, lower))
        like = upper * lax.rsqrt(jnp.maximum(lower, 0.02))
        return jnp.maximum(top, like), total + jnp.exp(like)

    top = jnp.full((cols, LANES), -jnp.inf, F32)
    top, total = lax.fori_loop(0, vels, visit, (top, jnp.zeros((cols, LANES), F32)), unroll=4)
    best_ref[...] = top
    score_ref[...] = jnp.log(total / vels)


def stack_epochs(where, shifts, pieces, cols, rows):
    vels = shifts.shape[0] // 2
    chips = len(pieces) // 2
    parts = pieces[0].shape[1] // LANES
    out = jax.ShapeDtypeStruct((cols, rows), F32)
    return pl.pallas_call(
        functools.partial(stack_kernel, chips, vels),
        out_shape=(out, out),
        in_specs=[SMEM] * 2 + [VMEM] * (2 * chips),
        out_specs=[VMEM] * 2,
        scratch_shapes=[pltpu.VMEM((2 * chips * parts * (cols + 2 * MAXSHIFT), LANES), F32)],
        compiler_params=PARAMS,
        name="stack",
    )(where, shifts, *pieces)


def on_device(image, inv_var, psf, shifts):
    epochs, width, rows = image.shape
    devices = lax.axis_size("space")
    row_blocks = lax.axis_size("tm")
    chips = devices // 2
    place, row_block = lax.axis_index("space"), lax.axis_index("tm")
    where = jnp.stack([place // 2, row_block, rows * row_blocks, place % 2]).astype(jnp.int32)
    table = jnp.transpose(shifts, (0, 2, 1)).reshape(2 * shifts.shape[0], shifts.shape[1])

    main, even, odd = prepare(image, inv_var)
    evens = [(i, i + 1) for i in range(0, row_blocks - 1, 2)]
    odds = [(i, i + 1) for i in range(1, row_blocks - 1, 2)]
    even = lax.ppermute(even, "tm", evens + [(j, i) for i, j in evens])
    odd = lax.ppermute(odd, "tm", odds + [(j, i) for i, j in odds])
    bands = band_matrices(psf, width // BLOCK)
    sent = filter_epochs(where, main, even, odd, bands, chips)

    swap = [(i, i ^ 1) for i in range(devices)]
    got = {0: sent[0]}
    for k in reversed(range(1, chips)):
        pairs = [(2 * i + c, 2 * (i ^ k) + c) for i in range(chips) for c in range(2)]
        got[k] = lax.ppermute(sent[k], "space", pairs)
    pieces = []
    for k in range(chips):
        pieces += [got[k], lax.ppermute(got[k], "space", swap)]
    return stack_epochs(where, table, pieces, width // devices, rows)


def solution(mesh):
    in_specs = (P("space", None, "tm"), P("space", None, "tm"), P(), P())
    out_specs = (P("space", "tm"), P("space", "tm"))
    return jax.shard_map(
        on_device, mesh=mesh, in_specs=in_specs, out_specs=out_specs, check_vma=False
    )
```

```python
import functools

import jax
import jax.numpy as jnp
from jax import lax
from jax.experimental import pallas as pl
from jax.experimental.pallas import tpu as pltpu
from jax.sharding import PartitionSpec as P

RADIUS = 7
TAPS = 2 * RADIUS + 1
MAXSHIFT = 16
LANES = 128
HALO = 24
BLOCK = 256
F32 = jnp.float32
BF16 = jnp.bfloat16
VMEM = pl.BlockSpec(memory_space=pltpu.VMEM)
SMEM = pl.BlockSpec(memory_space=pltpu.SMEM)
PARAMS = pltpu.CompilerParams(vmem_limit_bytes=24 * 1024 * 1024)


def prepare_kernel(weighted_ref, variance_ref, main_ref, even_ref, odd_ref):
    epochs, _, rows = weighted_ref.shape
    even = lax.rem(lax.axis_index("tm"), 2) == 0
    for ep in range(epochs):
        for plane, ref in ((0, weighted_ref), (1, variance_ref)):
            turned = ref[ep].astype(F32).T
            main_ref[plane, ep] = turned.astype(BF16)
            first, last = turned[:HALO], turned[rows - HALO :]
            even_ref[plane, ep] = jnp.where(even, last, first).astype(BF16)
            odd_ref[plane, ep] = jnp.where(even, first, last).astype(BF16)


def prepare(image, inv_var):
    epochs, width, rows = image.shape
    halo = jax.ShapeDtypeStruct((2, epochs, HALO, width), BF16)
    return pl.pallas_call(
        prepare_kernel,
        out_shape=(jax.ShapeDtypeStruct((2, epochs, rows, width), BF16), halo, halo),
        in_specs=[VMEM] * 2,
        out_specs=[VMEM] * 3,
        compiler_params=PARAMS,
        name="prepare",
    )((image * inv_var).astype(BF16), inv_var.astype(BF16))


def band_kernel(psf_ref, band_ref, *corner_refs):
    psf = psf_ref[...]
    normed = psf / jnp.sum(psf)
    flip = (
        lax.broadcasted_iota(jnp.int32, (TAPS, LANES), 0)
        + lax.broadcasted_iota(jnp.int32, (TAPS, LANES), 1)
        == TAPS - 1
    ).astype(BF16)
    size = (LANES, LANES)
    ahead = lax.broadcasted_iota(jnp.int32, size, 1) - lax.broadcasted_iota(jnp.int32, size, 0)
    near = jnp.abs(ahead) <= LANES // 2
    below = ahead > LANES // 2
    above = ahead < -(LANES // 2)
    for plane, kern in ((0, normed.astype(BF16)), (1, (normed * normed).astype(BF16))):
        taps = lax.dot_general(kern, flip, (((0,), (0,)), ((), ())), preferred_element_type=F32)
        for j in range(TAPS):
            spread = jnp.broadcast_to(taps[j : j + 1, :], size)
            ring = pltpu.roll(spread, LANES - RADIUS, 1, stride=1, stride_axis=0)
            diagonal = jnp.where(near, ring, 0.0).astype(BF16)
            at = j * BLOCK
            band_ref[plane, at : at + LANES, :LANES] = diagonal
            band_ref[plane, at + LANES : at + BLOCK, LANES:] = diagonal
            from_left = jnp.where(above, ring, 0.0).astype(BF16)
            from_right = jnp.where(below, ring, 0.0).astype(BF16)
            band_ref[plane, at : at + LANES, LANES:] = from_left
            band_ref[plane, at + LANES : at + BLOCK, :LANES] = from_right
            for corner_ref in corner_refs:
                corner_ref[plane, 0, j * LANES : (j + 1) * LANES] = from_left
                corner_ref[plane, 1, j * LANES : (j + 1) * LANES] = from_right


def band_matrices(psf, blocks):
    shapes = [jax.ShapeDtypeStruct((2, TAPS * BLOCK, BLOCK), BF16)]
    if blocks > 1:
        shapes.append(jax.ShapeDtypeStruct((2, 2, TAPS * LANES, LANES), BF16))
    return pl.pallas_call(
        band_kernel,
        out_shape=shapes,
        in_specs=[VMEM],
        out_specs=[VMEM] * len(shapes),
        compiler_params=PARAMS,
        name="band",
    )(psf)


def filter_kernel(chips, main_ref, even_ref, odd_ref, band_ref, *refs):
    blocks = main_ref.shape[3] // BLOCK
    if blocks > 1:
        corner_ref, refs = refs[0], refs[1:]
    outs, (tall, lhs, corner_lhs, turned, wide) = refs[:chips], refs[chips:]
    _, epochs, rows, width = main_ref.shape
    out_rows = rows + 2 * MAXSHIFT
    place, row_block = lax.axis_index("space"), lax.axis_index("tm")
    chip, core = lax.div(place, 2), lax.rem(place, 2)
    height = rows * lax.axis_size("tm")
    even = lax.rem(row_block, 2) == 0
    for plane in range(2):
        for ep in range(epochs):
            tall[plane, ep, HALO : HALO + rows] = main_ref[plane, ep]
    for is_even, before_ref, after_ref in ((True, odd_ref, even_ref), (False, even_ref, odd_ref)):

        @pl.when(even == is_even)
        def _():
            for plane in range(2):
                for ep in range(epochs):
                    tall[plane, ep, :HALO] = before_ref[plane, ep]
                    tall[plane, ep, HALO + rows :] = after_ref[plane, ep]

    row = row_block * rows - MAXSHIFT + lax.broadcasted_iota(jnp.int32, (out_rows, BLOCK), 0)
    inside = (row >= 0) & (row < height)
    skip = HALO - MAXSHIFT - RADIUS
    for block in range(blocks):
        at = block * BLOCK
        filtered = []
        for plane in range(2):
            for ep in range(epochs):
                for j in range(TAPS):
                    lhs[ep * out_rows : (ep + 1) * out_rows, j * BLOCK : (j + 1) * BLOCK] = tall[
                        plane, ep, skip + j : skip + j + out_rows, at : at + BLOCK
                    ]
            total = jnp.dot(lhs[...], band_ref[plane], preferred_element_type=F32)
            low, high = total[:, :LANES], total[:, LANES:]
            for side, source in ((0, at - LANES), (1, at + BLOCK)):
                if source < 0 or source >= width:
                    continue
                for ep in range(epochs):
                    for j in range(TAPS):
                        corner_lhs[ep * out_rows : (ep + 1) * out_rows, j * LANES : (j + 1) * LANES] = tall[
                            plane, ep, skip + j : skip + j + out_rows, source : source + LANES
                        ]
                more = jnp.dot(corner_lhs[...], corner_ref[plane, side], preferred_element_type=F32)
                low, high = (low + more, high) if side == 0 else (low, high + more)
            total = jnp.concatenate([low, high], axis=1)
            parts = []
            for ep in range(epochs):
                part = total[ep * out_rows : (ep + 1) * out_rows]
                parts.append(jnp.where(inside, part.astype(BF16).astype(F32), 0.0))
            filtered.append(parts)
        for ep in range(epochs):
            psi, phi = filtered[0][ep], filtered[1][ep]
            signal = jnp.abs(psi) * lax.rsqrt(jnp.maximum(phi, 0.001))
            weight = 1.0 / (1.0 + jnp.exp(2.0 * signal - 4.0))
            for plane, values in ((0, weight * psi), (1, weight * phi)):
                slot = 2 * ep + plane
                turn = (MAXSHIFT * 2 * slot) % rows
                base = slot * LANES
                turned[base + turn : base + rows, :] = values[: rows - turn]
                if turn:
                    turned[base : base + turn, :] = values[rows - turn : rows]
                extra = 2 * epochs * LANES + slot * 2 * MAXSHIFT
                turned[extra : extra + 2 * MAXSHIFT, :] = values[rows:]
        for part in range(2 * epochs + 1):
            lanes = slice(part * LANES, (part + 1) * LANES)
            wide[MAXSHIFT + at : MAXSHIFT + at + BLOCK, lanes] = turned[lanes, :].T.astype(BF16)
    edge = jnp.zeros((MAXSHIFT, wide.shape[1]), BF16)
    wide[:MAXSHIFT] = edge
    wide[MAXSHIFT + width :] = edge
    span = width // chips
    cols = span // 2
    for k in range(chips):
        other = jnp.bitwise_xor(chip, k)
        start = other * span
        for third in range(3):
            rows_from = start + lax.rem(third + 2 * core, 3) * cols
            outs[k][third * cols : (third + 1) * cols] = wide[
                pl.ds(pl.multiple_of(rows_from, cols), cols), :
            ]


def filter_epochs(main, even, odd, bands, chips):
    _, epochs, rows, width = main.shape
    out_rows = rows + 2 * MAXSHIFT
    lanes = (2 * epochs + 1) * LANES
    piece = jax.ShapeDtypeStruct((width // chips + 2 * MAXSHIFT, lanes), BF16)
    return pl.pallas_call(
        functools.partial(filter_kernel, chips),
        out_shape=(piece,) * chips,
        in_specs=[VMEM] * (3 + len(bands)),
        out_specs=[VMEM] * chips,
        scratch_shapes=[
            pltpu.VMEM((2, epochs, rows + 2 * HALO, width), BF16),
            pltpu.VMEM((epochs * out_rows, TAPS * BLOCK), BF16),
            pltpu.VMEM((epochs * out_rows, TAPS * LANES), BF16),
            pltpu.VMEM((lanes, BLOCK), F32),
            pltpu.VMEM((width + 2 * MAXSHIFT, lanes), BF16),
        ],
        compiler_params=PARAMS,
        name="filter",
    )(main, even, odd, *bands)


def stack_kernel(members, vels, first, final, shifts_ref, *refs):
    count = 2 * len(members)
    pieces, refs, frames = refs[:count], refs[count:-1], refs[-1]
    if not first:
        start_ref, refs = refs[0], refs[1:]
    place = lax.axis_index("space")
    chip, core = lax.div(place, 2), lax.rem(place, 2)
    cols = refs[0].shape[-2]
    window = cols + 2 * MAXSHIFT
    parts = pieces[0].shape[1] // LANES
    epochs = (parts - 1) // 2
    for slot in range(count):
        for half in range(2):
            own = 2 * cols * core if half == 0 else cols * (1 - core)
            start = pl.multiple_of(own, cols) if slot % 2 == 0 else half * cols
            for part in range(parts):
                base = (slot * parts + part) * window + half * cols
                frames[base : base + cols] = pieces[slot][
                    pl.ds(start, cols), part * LANES : (part + 1) * LANES
                ].astype(F32)
    lane = lax.broadcasted_iota(jnp.int32, (cols, LANES), 1)

    def add_slot(slot, k, flip, v, upper, lower):
        owner = 2 * jnp.bitwise_xor(chip, k) + jnp.bitwise_xor(core, flip)
        for ep in range(epochs):
            epoch = owner * epochs + ep
            right = MAXSHIFT + shifts_ref[2 * v, epoch]
            down = MAXSHIFT + shifts_ref[2 * v + 1, epoch]
            base = slot * (parts * window) + right
            extra = frames[pl.ds(base + 2 * epochs * window, cols), :]
            sums = []
            for plane, total in ((0, upper), (1, lower)):
                part = 2 * ep + plane
                turn = 2 * MAXSHIFT * part
                spot = lane if turn == 0 else lax.rem(lane + (LANES - turn), LANES)
                held = frames[pl.ds(base + part * window, cols), :]
                merged = jnp.where(spot < down, extra, held)
                sums.append(total + pltpu.roll(merged, lax.rem(2 * LANES - turn - down, LANES), 1))
            upper, lower = sums
        return upper, lower

    def add_all(v):
        if first:
            sums = (jnp.zeros((cols, LANES), F32), jnp.zeros((cols, LANES), F32))
        else:
            sums = (start_ref[v, 0], start_ref[v, 1])
        for i, k in enumerate(members):
            for flip in range(2):
                sums = add_slot(2 * i + flip, k, flip, v, *sums)
        return sums

    unroll = vels if len(members) <= 4 else 1
    if final:
        best_ref, score_ref = refs

        def visit(v, carry):
            top, total = carry
            upper, lower = add_all(v)
            like = upper * lax.rsqrt(jnp.maximum(lower, 0.02))
            return jnp.maximum(top, like), total + jnp.exp(like)

        top = jnp.full((cols, LANES), -jnp.inf, F32)
        top, total = lax.fori_loop(0, vels, visit, (top, jnp.zeros((cols, LANES), F32)), unroll=unroll)
        best_ref[...] = top
        score_ref[...] = jnp.log(total / vels)
    else:
        (sum_ref,) = refs

        def keep(v, carry):
            sum_ref[v, 0], sum_ref[v, 1] = add_all(v)
            return carry

        lax.fori_loop(0, vels, keep, 0, unroll=unroll)


def stack_epochs(shifts, members, pieces, sums, final, cols, rows):
    vels = shifts.shape[0] // 2
    parts = pieces[0].shape[1] // LANES
    if final:
        out_shape = (jax.ShapeDtypeStruct((cols, rows), F32),) * 2
    else:
        out_shape = (jax.ShapeDtypeStruct((vels, 2, cols, rows), F32),)
    return pl.pallas_call(
        functools.partial(stack_kernel, members, vels, not sums, final),
        out_shape=out_shape,
        in_specs=[SMEM] + [VMEM] * (len(pieces) + len(sums)),
        out_specs=[VMEM] * len(out_shape),
        scratch_shapes=[pltpu.VMEM((len(pieces) * parts * (cols + 2 * MAXSHIFT), LANES), F32)],
        compiler_params=PARAMS,
        name="stack_end" if final else "stack_part",
    )(shifts, *pieces, *sums)


def on_device(image, inv_var, psf, shifts):
    epochs, width, rows = image.shape
    devices = lax.axis_size("space")
    row_blocks = lax.axis_size("tm")
    chips = devices // 2
    table = jnp.transpose(shifts, (0, 2, 1)).reshape(2 * shifts.shape[0], shifts.shape[1])

    main, even, odd = prepare(image, inv_var)
    evens = [(i, i + 1) for i in range(0, row_blocks - 1, 2)]
    odds = [(i, i + 1) for i in range(1, row_blocks - 1, 2)]
    even = lax.ppermute(even, "tm", evens + [(j, i) for i, j in evens])
    odd = lax.ppermute(odd, "tm", odds + [(j, i) for i, j in odds])
    bands = band_matrices(psf, width // BLOCK)
    sent = filter_epochs(main, even, odd, bands, chips)

    swap = [(i, i ^ 1) for i in range(devices)]
    cols = width // devices

    got = {0: sent[0]}
    for k in range(1, chips):
        pairs = [(2 * i + c, 2 * (i ^ k) + c) for i in range(chips) for c in range(2)]
        got[k] = lax.ppermute(sent[k], "space", pairs)
    last = chips // 2
    first = tuple(k for k in reversed(range(chips)) if k not in (1, last))
    steps = (first, (1,), (last,)) if last > 1 else (first, (last,))
    sums = ()
    for step, members in enumerate(steps):
        if step == 1:
            got[last], sums = lax.optimization_barrier((got[last], sums))
        pieces = []
        for k in members:
            pieces += [got[k], lax.ppermute(got[k][cols:], "space", swap)]
        sums = stack_epochs(table, members, pieces, sums, members == (last,), cols, rows)
    return sums


def solution(mesh):
    in_specs = (P("space", None, "tm"), P("space", None, "tm"), P(), P())
    out_specs = (P("space", "tm"), P("space", "tm"))
    return jax.shard_map(
        on_device, mesh=mesh, in_specs=in_specs, out_specs=out_specs, check_vma=False
    )
```

```python
import functools

import jax
import jax.numpy as jnp
from jax import lax
from jax.experimental import pallas as pl
from jax.experimental.pallas import tpu as pltpu
from jax.sharding import PartitionSpec as P

RADIUS = 7
TAPS = 2 * RADIUS + 1
MAXSHIFT = 16
LANES = 128
HALO = 24
BLOCK = 256
F32 = jnp.float32
BF16 = jnp.bfloat16
VMEM = pl.BlockSpec(memory_space=pltpu.VMEM)
ANY = pl.BlockSpec(memory_space=pl.ANY)
PARAMS = pltpu.CompilerParams(vmem_limit_bytes=24 * 1024 * 1024)


def prepare_kernel(image_hbm, inv_var_hbm, psf_hbm, main_ref, even_ref, odd_ref, psf_ref, image, inv_var, sems):
    epochs, _, rows = image.shape
    copies = []
    for ep in range(epochs):
        for i, (source, target) in enumerate(((image_hbm, image), (inv_var_hbm, inv_var))):
            copies.append(pltpu.make_async_copy(source.at[ep], target.at[ep], sems.at[ep, i]))
            copies[-1].start()
    psf_copy = pltpu.make_async_copy(psf_hbm, psf_ref, sems.at[epochs, 0])
    psf_copy.start()
    even = lax.rem(lax.axis_index("tm"), 2) == 0
    for ep in range(epochs):
        for copy in copies[2 * ep : 2 * ep + 2]:
            copy.wait()
        for plane, values in ((0, image[ep] * inv_var[ep]), (1, inv_var[ep])):
            turned = values.T
            main_ref[plane, ep] = turned.astype(BF16)
            first, last = turned[:HALO], turned[rows - HALO :]
            even_ref[plane, ep] = jnp.where(even, last, first).astype(BF16)
            odd_ref[plane, ep] = jnp.where(even, first, last).astype(BF16)
    psf_copy.wait()


def prepare(image, inv_var, psf):
    epochs, width, rows = image.shape
    halo = jax.ShapeDtypeStruct((2, epochs, HALO, width), BF16)
    return pl.pallas_call(
        prepare_kernel,
        out_shape=(
            jax.ShapeDtypeStruct((2, epochs, rows, width), BF16),
            halo,
            halo,
            jax.ShapeDtypeStruct(psf.shape, F32),
        ),
        in_specs=[ANY] * 3,
        out_specs=[VMEM] * 4,
        scratch_shapes=[
            pltpu.VMEM(image.shape, F32),
            pltpu.VMEM(image.shape, F32),
            pltpu.SemaphoreType.DMA((epochs + 1, 2)),
        ],
        compiler_params=PARAMS,
        name="prepare",
    )(*(pltpu.with_memory_space_constraint(array, pltpu.HBM) for array in (image, inv_var, psf)))


def band_kernel(psf_ref, band_ref, *corner_refs):
    psf = psf_ref[...]
    normed = psf / jnp.sum(psf)
    flip = (
        lax.broadcasted_iota(jnp.int32, (TAPS, LANES), 0)
        + lax.broadcasted_iota(jnp.int32, (TAPS, LANES), 1)
        == TAPS - 1
    ).astype(BF16)
    size = (LANES, LANES)
    ahead = lax.broadcasted_iota(jnp.int32, size, 1) - lax.broadcasted_iota(jnp.int32, size, 0)
    near = jnp.abs(ahead) <= LANES // 2
    below = ahead > LANES // 2
    above = ahead < -(LANES // 2)
    for plane, kern in ((0, normed.astype(BF16)), (1, (normed * normed).astype(BF16))):
        taps = lax.dot_general(kern, flip, (((0,), (0,)), ((), ())), preferred_element_type=F32)
        for j in range(TAPS):
            spread = jnp.broadcast_to(taps[j : j + 1, :], size)
            ring = pltpu.roll(spread, LANES - RADIUS, 1, stride=1, stride_axis=0)
            diagonal = jnp.where(near, ring, 0.0).astype(BF16)
            at = j * BLOCK
            band_ref[plane, at : at + LANES, :LANES] = diagonal
            band_ref[plane, at + LANES : at + BLOCK, LANES:] = diagonal
            from_left = jnp.where(above, ring, 0.0).astype(BF16)
            from_right = jnp.where(below, ring, 0.0).astype(BF16)
            band_ref[plane, at : at + LANES, LANES:] = from_left
            band_ref[plane, at + LANES : at + BLOCK, :LANES] = from_right
            for corner_ref in corner_refs:
                corner_ref[plane, 0, j * LANES : (j + 1) * LANES] = from_left
                corner_ref[plane, 1, j * LANES : (j + 1) * LANES] = from_right


def band_matrices(psf, blocks):
    shapes = [jax.ShapeDtypeStruct((2, TAPS * BLOCK, BLOCK), BF16)]
    if blocks > 1:
        shapes.append(jax.ShapeDtypeStruct((2, 2, TAPS * LANES, LANES), BF16))
    return pl.pallas_call(
        band_kernel,
        out_shape=shapes,
        in_specs=[VMEM],
        out_specs=[VMEM] * len(shapes),
        compiler_params=PARAMS,
        name="band",
    )(psf)


def filter_rows(sources, skip, count, at, lhs, corner_lhs, band_ref, corner_ref, plane):
    width = sources[0].shape[1]
    for i, source in enumerate(sources):
        for j in range(TAPS):
            lhs[i * count : (i + 1) * count, j * BLOCK : (j + 1) * BLOCK] = source[
                skip + j : skip + j + count, at : at + BLOCK
            ]
    total = jnp.dot(lhs[...], band_ref[plane], preferred_element_type=F32)
    low, high = total[:, :LANES], total[:, LANES:]
    for side, start in ((0, at - LANES), (1, at + BLOCK)):
        if start < 0 or start >= width:
            continue
        for i, source in enumerate(sources):
            for j in range(TAPS):
                corner_lhs[i * count : (i + 1) * count, j * LANES : (j + 1) * LANES] = source[
                    skip + j : skip + j + count, start : start + LANES
                ]
        more = jnp.dot(corner_lhs[...], corner_ref[plane, side], preferred_element_type=F32)
        low, high = (low + more, high) if side == 0 else (low, high + more)
    total = jnp.concatenate([low, high], axis=1).astype(BF16).astype(F32)
    return [total[i * count : (i + 1) * count] for i in range(len(sources))]


def weigh(psi, phi):
    signal = jnp.abs(psi) * lax.rsqrt(jnp.maximum(phi, 0.001))
    weight = 1.0 / (1.0 + jnp.exp(2.0 * signal - 4.0))
    return weight * psi, weight * phi


def middle_kernel(main_ref, band_ref, *refs):
    corner_ref, out_ref, (lhs, corner_lhs) = (refs[0] if len(refs) > 3 else None), refs[-3], refs[-2:]
    _, epochs, rows, width = main_ref.shape
    for at in range(0, width, BLOCK):
        psi, phi = (
            filter_rows(
                [main_ref.at[plane, ep] for ep in range(epochs)],
                MAXSHIFT - RADIUS, rows - 2 * MAXSHIFT, at, lhs, corner_lhs, band_ref, corner_ref, plane,
            )
            for plane in range(2)
        )
        for ep in range(epochs):
            out_ref[2 * ep, :, at : at + BLOCK], out_ref[2 * ep + 1, :, at : at + BLOCK] = weigh(psi[ep], phi[ep])


def filter_middle(main, bands):
    _, epochs, rows, width = main.shape
    inner = rows - 2 * MAXSHIFT
    return pl.pallas_call(
        middle_kernel,
        out_shape=jax.ShapeDtypeStruct((2 * epochs, inner, width), F32),
        in_specs=[VMEM] * (1 + len(bands)),
        out_specs=VMEM,
        scratch_shapes=[
            pltpu.VMEM((epochs * inner, TAPS * BLOCK), BF16),
            pltpu.VMEM((epochs * inner, TAPS * LANES), BF16),
        ],
        compiler_params=PARAMS,
        name="middle",
    )(main, *bands)


def border_kernel(chips, main_ref, odd_ref, even_ref, middle_ref, band_ref, *refs):
    corner_ref, refs = (refs[0], refs[1:]) if main_ref.shape[3] > BLOCK else (None, refs)
    outs, (ends, lhs, corner_lhs, turned, wide) = refs[:chips], refs[chips:]
    _, epochs, rows, width = main_ref.shape
    place, row_block = lax.axis_index("space"), lax.axis_index("tm")
    chip, core = lax.div(place, 2), lax.rem(place, 2)
    even = lax.rem(row_block, 2) == 0
    for plane in range(2):
        for ep in range(epochs):
            before = jnp.where(even, odd_ref[plane, ep].astype(F32), even_ref[plane, ep].astype(F32))
            after = jnp.where(even, even_ref[plane, ep].astype(F32), odd_ref[plane, ep].astype(F32))
            first = main_ref[plane, ep, :HALO].astype(F32)
            last = main_ref[plane, ep, rows - HALO :].astype(F32)
            ends[plane, ep] = jnp.concatenate([before, first], axis=0).astype(BF16)
            ends[plane, epochs + ep] = jnp.concatenate([last, after], axis=0).astype(BF16)
    span = 2 * MAXSHIFT
    row = lax.broadcasted_iota(jnp.int32, (span, BLOCK), 0)
    above = (row_block > 0) | (row >= MAXSHIFT)
    below = (row_block < lax.axis_size("tm") - 1) | (row < MAXSHIFT)
    for at in range(0, width, BLOCK):
        psi, phi = (
            filter_rows(
                [ends.at[plane, i] for i in range(2 * epochs)],
                HALO - MAXSHIFT - RADIUS, span, at, lhs, corner_lhs, band_ref, corner_ref, plane,
            )
            for plane in range(2)
        )
        for i in range(2 * epochs):
            ep, inside = i % epochs, (above if i < epochs else below)
            values = weigh(psi[i], phi[i])
            for plane in range(2):
                slot = 2 * ep + plane
                turn = (span * slot) % rows
                held = jnp.where(inside, values[plane], 0.0)
                if i < epochs:
                    base = slot * LANES
                    turned[base + turn : base + turn + span, :] = held
                    inner = middle_ref[slot, :, at : at + BLOCK]
                    straight = rows - span - turn
                    if straight:
                        turned[base + turn + span : base + rows, :] = inner[:straight]
                    if turn:
                        turned[base : base + turn, :] = inner[straight:]
                else:
                    extra = 2 * epochs * LANES + slot * span
                    turned[extra : extra + span, :] = held
        for part in range(2 * epochs + 1):
            lanes = slice(part * LANES, (part + 1) * LANES)
            wide[MAXSHIFT + at : MAXSHIFT + at + BLOCK, lanes] = turned[lanes, :].T.astype(BF16)
    edge = jnp.zeros((MAXSHIFT, wide.shape[1]), BF16)
    wide[:MAXSHIFT] = edge
    wide[MAXSHIFT + width :] = edge
    cols = width // chips // 2
    for k in range(chips):
        start = jnp.bitwise_xor(chip, k) * (2 * cols)
        for third in range(3):
            rows_from = start + lax.rem(third + 2 * core, 3) * cols
            outs[k][third * cols : (third + 1) * cols] = wide[pl.ds(pl.multiple_of(rows_from, cols), cols), :]


def filter_border(main, odd, even, middle, bands, chips):
    _, epochs, rows, width = main.shape
    lanes = (2 * epochs + 1) * LANES
    span = 2 * MAXSHIFT
    piece = jax.ShapeDtypeStruct((width // chips + span, lanes), BF16)
    return pl.pallas_call(
        functools.partial(border_kernel, chips),
        out_shape=(piece,) * chips,
        in_specs=[VMEM] * (4 + len(bands)),
        out_specs=[VMEM] * chips,
        scratch_shapes=[
            pltpu.VMEM((2, 2 * epochs, 2 * HALO, width), BF16),
            pltpu.VMEM((2 * epochs * span, TAPS * BLOCK), BF16),
            pltpu.VMEM((2 * epochs * span, TAPS * LANES), BF16),
            pltpu.VMEM((lanes, BLOCK), F32),
            pltpu.VMEM((width + span, lanes), BF16),
        ],
        compiler_params=PARAMS,
        name="border",
    )(main, odd, even, middle, *bands)


def stack_kernel(members, vels, first, final, shifts_hbm, *refs):
    count = 2 * len(members)
    scratch = 5 if final else 3
    pieces, refs, scratch = refs[:count], refs[count:-scratch], refs[-scratch:]
    frames, shifts_ref, sems = scratch[:3]
    table = pltpu.make_async_copy(shifts_hbm, shifts_ref, sems.at[0])
    table.start()
    if not first:
        start_ref, refs = refs[0], refs[1:]
    place = lax.axis_index("space")
    chip, core = lax.div(place, 2), lax.rem(place, 2)
    cols = refs[-1].shape[-2]
    window = cols + 2 * MAXSHIFT
    parts = pieces[0].shape[1] // LANES
    epochs = (parts - 1) // 2
    for slot in range(count):
        for half in range(2):
            own = 2 * cols * core if half == 0 else cols * (1 - core)
            start = pl.multiple_of(own, cols) if slot % 2 == 0 else half * cols
            for part in range(parts):
                base = (slot * parts + part) * window + half * cols
                frames[base : base + cols] = pieces[slot][
                    pl.ds(start, cols), part * LANES : (part + 1) * LANES
                ].astype(F32)
    table.wait()
    lane = lax.broadcasted_iota(jnp.int32, (cols, LANES), 1)

    def add_slot(slot, k, flip, v, upper, lower):
        owner = 2 * jnp.bitwise_xor(chip, k) + jnp.bitwise_xor(core, flip)
        for ep in range(epochs):
            epoch = owner * epochs + ep
            right = MAXSHIFT + shifts_ref[2 * v, epoch]
            down = MAXSHIFT + shifts_ref[2 * v + 1, epoch]
            base = slot * (parts * window) + right
            extra = frames[pl.ds(base + 2 * epochs * window, cols), :]
            sums = []
            for plane, total in ((0, upper), (1, lower)):
                part = 2 * ep + plane
                turn = 2 * MAXSHIFT * part
                spot = lane if turn == 0 else lax.rem(lane + (LANES - turn), LANES)
                held = frames[pl.ds(base + part * window, cols), :]
                merged = jnp.where(spot < down, extra, held)
                sums.append(total + pltpu.roll(merged, lax.rem(2 * LANES - turn - down, LANES), 1))
            upper, lower = sums
        return upper, lower

    def add_all(v):
        if first:
            sums = (jnp.zeros((cols, LANES), F32), jnp.zeros((cols, LANES), F32))
        else:
            sums = (start_ref[v, 0], start_ref[v, 1])
        for i, k in enumerate(members):
            for flip in range(2):
                sums = add_slot(2 * i + flip, k, flip, v, *sums)
        return sums

    unroll = vels if len(members) <= 4 else 1
    if final:
        best_ref, score_ref = refs

        def visit(v, carry):
            top, total = carry
            upper, lower = add_all(v)
            like = upper * lax.rsqrt(jnp.maximum(lower, 0.02))
            return jnp.maximum(top, like), total + jnp.exp(like)

        top = jnp.full((cols, LANES), -jnp.inf, F32)
        top, total = lax.fori_loop(0, vels, visit, (top, jnp.zeros((cols, LANES), F32)), unroll=unroll)
        best, score = scratch[3:]
        best[...] = top
        best_copy = pltpu.make_async_copy(best, best_ref, sems.at[1])
        best_copy.start()
        score[...] = jnp.log(total / vels)
        score_copy = pltpu.make_async_copy(score, score_ref, sems.at[2])
        score_copy.start()
        best_copy.wait()
        score_copy.wait()
    else:
        (sum_ref,) = refs

        def keep(v, carry):
            sum_ref[v, 0], sum_ref[v, 1] = add_all(v)
            return carry

        lax.fori_loop(0, vels, keep, 0, unroll=unroll)


def stack_epochs(shifts, members, pieces, sums, final, cols, rows):
    vels = shifts.shape[0] // 2
    parts = pieces[0].shape[1] // LANES
    if final:
        out_shape = (jax.ShapeDtypeStruct((cols, rows), F32),) * 2
    else:
        out_shape = (jax.ShapeDtypeStruct((vels, 2, cols, rows), F32),)
    scratch = [
        pltpu.VMEM((len(pieces) * parts * (cols + 2 * MAXSHIFT), LANES), F32),
        pltpu.SMEM(shifts.shape, jnp.int32),
        pltpu.SemaphoreType.DMA((3,)),
    ]
    if final:
        scratch += [pltpu.VMEM((cols, rows), F32)] * 2
    return pl.pallas_call(
        functools.partial(stack_kernel, members, vels, not sums, final),
        out_shape=out_shape,
        in_specs=[ANY] + [VMEM] * (len(pieces) + len(sums)),
        out_specs=[ANY if final else VMEM] * len(out_shape),
        scratch_shapes=scratch,
        compiler_params=PARAMS,
        name="stack_end" if final else "stack_part",
    )(shifts, *pieces, *sums)


def on_device(image, inv_var, psf, shifts):
    epochs, width, rows = image.shape
    devices = lax.axis_size("space")
    row_blocks = lax.axis_size("tm")
    chips = devices // 2
    table = jnp.transpose(shifts, (0, 2, 1)).reshape(2 * shifts.shape[0], shifts.shape[1])

    main, even, odd, psf = prepare(image, inv_var, psf)
    evens = [(i, i + 1) for i in range(0, row_blocks - 1, 2)]
    odds = [(i, i + 1) for i in range(1, row_blocks - 1, 2)]
    even = lax.ppermute(even, "tm", evens + [(j, i) for i, j in evens])
    odd = lax.ppermute(odd, "tm", odds + [(j, i) for i, j in odds])
    bands = band_matrices(psf, width // BLOCK)
    middle = filter_middle(main, bands)
    sent = filter_border(main, odd, even, middle, bands, chips)

    swap = [(i, i ^ 1) for i in range(devices)]
    cols = width // devices

    got = {0: sent[0]}
    for k in range(1, chips):
        pairs = [(2 * i + c, 2 * (i ^ k) + c) for i in range(chips) for c in range(2)]
        got[k] = lax.ppermute(sent[k], "space", pairs)
    last = chips // 2
    first = tuple(k for k in reversed(range(chips)) if k not in (1, last))
    steps = (first, (1,), (last,)) if last > 1 else (first, (last,))
    sums = ()
    for step, members in enumerate(steps):
        if step == 1:
            got[last], sums = lax.optimization_barrier((got[last], sums))
        pieces = []
        for k in members:
            pieces += [got[k], lax.ppermute(got[k][cols:], "space", swap)]
        sums = stack_epochs(table, members, pieces, sums, members == (last,), cols, rows)
    return sums


def solution(mesh):
    in_specs = (P("space", None, "tm"), P("space", None, "tm"), P(), P())
    out_specs = (P("space", "tm"), P("space", "tm"))
    return jax.shard_map(
        on_device, mesh=mesh, in_specs=in_specs, out_specs=out_specs, check_vma=False
    )
```

```python
import functools

import jax
import jax.numpy as jnp
from jax import lax
from jax.experimental import pallas as pl
from jax.experimental.pallas import tpu as pltpu
from jax.sharding import PartitionSpec as P

RADIUS = 7
TAPS = 2 * RADIUS + 1
MAXSHIFT = 16
LANES = 128
HALO = 24
BLOCK = 256
F32 = jnp.float32
BF16 = jnp.bfloat16
VMEM = pl.BlockSpec(memory_space=pltpu.VMEM)
ANY = pl.BlockSpec(memory_space=pl.ANY)
PARAMS = pltpu.CompilerParams(vmem_limit_bytes=24 * 1024 * 1024)


def prepare_kernel(image_hbm, inv_var_hbm, psf_hbm, main_ref, even_ref, odd_ref, psf_ref, image, inv_var, sems):
    epochs, _, rows = image.shape
    copies = []
    for ep in range(epochs):
        for i, (source, target) in enumerate(((image_hbm, image), (inv_var_hbm, inv_var))):
            copies.append(pltpu.make_async_copy(source.at[ep], target.at[ep], sems.at[ep, i]))
            copies[-1].start()
    psf_copy = pltpu.make_async_copy(psf_hbm, psf_ref, sems.at[epochs, 0])
    psf_copy.start()
    even = lax.rem(lax.axis_index("tm"), 2) == 0
    for ep in range(epochs):
        for copy in copies[2 * ep : 2 * ep + 2]:
            copy.wait()
        for plane, values in ((0, image[ep] * inv_var[ep]), (1, inv_var[ep])):
            turned = values.T
            main_ref[plane, ep] = turned.astype(BF16)
            first, last = turned[:HALO], turned[rows - HALO :]
            even_ref[plane, ep] = jnp.where(even, last, first).astype(BF16)
            odd_ref[plane, ep] = jnp.where(even, first, last).astype(BF16)
    psf_copy.wait()


def prepare(image, inv_var, psf):
    epochs, width, rows = image.shape
    halo = jax.ShapeDtypeStruct((2, epochs, HALO, width), BF16)
    return pl.pallas_call(
        prepare_kernel,
        out_shape=(
            jax.ShapeDtypeStruct((2, epochs, rows, width), BF16),
            halo,
            halo,
            jax.ShapeDtypeStruct(psf.shape, F32),
        ),
        in_specs=[ANY] * 3,
        out_specs=[VMEM] * 4,
        scratch_shapes=[
            pltpu.VMEM(image.shape, F32),
            pltpu.VMEM(image.shape, F32),
            pltpu.SemaphoreType.DMA((epochs + 1, 2)),
        ],
        compiler_params=PARAMS,
        name="prepare",
    )(*(pltpu.with_memory_space_constraint(array, pltpu.HBM) for array in (image, inv_var, psf)))


def band_kernel(psf_ref, band_ref, *corner_refs):
    psf = psf_ref[...]
    normed = psf / jnp.sum(psf)
    flip = (
        lax.broadcasted_iota(jnp.int32, (TAPS, LANES), 0)
        + lax.broadcasted_iota(jnp.int32, (TAPS, LANES), 1)
        == TAPS - 1
    ).astype(BF16)
    size = (LANES, LANES)
    ahead = lax.broadcasted_iota(jnp.int32, size, 1) - lax.broadcasted_iota(jnp.int32, size, 0)
    near = jnp.abs(ahead) <= LANES // 2
    below = ahead > LANES // 2
    above = ahead < -(LANES // 2)
    for plane, kern in ((0, normed.astype(BF16)), (1, (normed * normed).astype(BF16))):
        taps = lax.dot_general(kern, flip, (((0,), (0,)), ((), ())), preferred_element_type=F32)
        for j in range(TAPS):
            spread = jnp.broadcast_to(taps[j : j + 1, :], size)
            ring = pltpu.roll(spread, LANES - RADIUS, 1, stride=1, stride_axis=0)
            diagonal = jnp.where(near, ring, 0.0).astype(BF16)
            at = j * BLOCK
            band_ref[plane, at : at + LANES, :LANES] = diagonal
            band_ref[plane, at + LANES : at + BLOCK, LANES:] = diagonal
            from_left = jnp.where(above, ring, 0.0).astype(BF16)
            from_right = jnp.where(below, ring, 0.0).astype(BF16)
            band_ref[plane, at : at + LANES, LANES:] = from_left
            band_ref[plane, at + LANES : at + BLOCK, :LANES] = from_right
            for corner_ref in corner_refs:
                corner_ref[plane, 0, j * LANES : (j + 1) * LANES] = from_left
                corner_ref[plane, 1, j * LANES : (j + 1) * LANES] = from_right


def band_matrices(psf, blocks):
    shapes = [jax.ShapeDtypeStruct((2, TAPS * BLOCK, BLOCK), BF16)]
    if blocks > 1:
        shapes.append(jax.ShapeDtypeStruct((2, 2, TAPS * LANES, LANES), BF16))
    return pl.pallas_call(
        band_kernel,
        out_shape=shapes,
        in_specs=[VMEM],
        out_specs=[VMEM] * len(shapes),
        compiler_params=PARAMS,
        name="band",
    )(psf)


def filter_rows(sources, skip, count, at, lhs, corner_lhs, band_ref, corner_ref, plane):
    width = sources[0].shape[1]
    for i, source in enumerate(sources):
        for j in range(TAPS):
            lhs[i * count : (i + 1) * count, j * BLOCK : (j + 1) * BLOCK] = source[
                skip + j : skip + j + count, at : at + BLOCK
            ]
    total = jnp.dot(lhs[...], band_ref[plane], preferred_element_type=F32)
    low, high = total[:, :LANES], total[:, LANES:]
    for side, start in ((0, at - LANES), (1, at + BLOCK)):
        if start < 0 or start >= width:
            continue
        for i, source in enumerate(sources):
            for j in range(TAPS):
                corner_lhs[i * count : (i + 1) * count, j * LANES : (j + 1) * LANES] = source[
                    skip + j : skip + j + count, start : start + LANES
                ]
        more = jnp.dot(corner_lhs[...], corner_ref[plane, side], preferred_element_type=F32)
        low, high = (low + more, high) if side == 0 else (low, high + more)
    total = jnp.concatenate([low, high], axis=1).astype(BF16).astype(F32)
    return [total[i * count : (i + 1) * count] for i in range(len(sources))]


def weigh(psi, phi):
    signal = jnp.abs(psi) * lax.rsqrt(jnp.maximum(phi, 0.001))
    weight = 1.0 / (1.0 + jnp.exp(2.0 * signal - 4.0))
    return weight * psi, weight * phi


def middle_kernel(main_ref, band_ref, *refs):
    corner_ref, out_ref, (lhs, corner_lhs) = (refs[0] if len(refs) > 3 else None), refs[-3], refs[-2:]
    _, epochs, rows, width = main_ref.shape
    for at in range(0, width, BLOCK):
        psi, phi = (
            filter_rows(
                [main_ref.at[plane, ep] for ep in range(epochs)],
                MAXSHIFT - RADIUS, rows - 2 * MAXSHIFT, at, lhs, corner_lhs, band_ref, corner_ref, plane,
            )
            for plane in range(2)
        )
        for ep in range(epochs):
            out_ref[2 * ep, :, at : at + BLOCK], out_ref[2 * ep + 1, :, at : at + BLOCK] = weigh(psi[ep], phi[ep])


def filter_middle(main, bands):
    _, epochs, rows, width = main.shape
    inner = rows - 2 * MAXSHIFT
    return pl.pallas_call(
        middle_kernel,
        out_shape=jax.ShapeDtypeStruct((2 * epochs, inner, width), F32),
        in_specs=[VMEM] * (1 + len(bands)),
        out_specs=VMEM,
        scratch_shapes=[
            pltpu.VMEM((epochs * inner, TAPS * BLOCK), BF16),
            pltpu.VMEM((epochs * inner, TAPS * LANES), BF16),
        ],
        compiler_params=PARAMS,
        name="middle",
    )(main, *bands)


def border_kernel(chips, main_ref, odd_ref, even_ref, middle_ref, band_ref, *refs):
    corner_ref, refs = (refs[0], refs[1:]) if main_ref.shape[3] > BLOCK else (None, refs)
    outs, (ends, lhs, corner_lhs, turned, wide) = refs[:chips], refs[chips:]
    _, epochs, rows, width = main_ref.shape
    place, row_block = lax.axis_index("space"), lax.axis_index("tm")
    chip, core = lax.div(place, 2), lax.rem(place, 2)
    even = lax.rem(row_block, 2) == 0
    for plane in range(2):
        for ep in range(epochs):
            before = jnp.where(even, odd_ref[plane, ep].astype(F32), even_ref[plane, ep].astype(F32))
            after = jnp.where(even, even_ref[plane, ep].astype(F32), odd_ref[plane, ep].astype(F32))
            first = main_ref[plane, ep, :HALO].astype(F32)
            last = main_ref[plane, ep, rows - HALO :].astype(F32)
            ends[plane, ep] = jnp.concatenate([before, first], axis=0).astype(BF16)
            ends[plane, epochs + ep] = jnp.concatenate([last, after], axis=0).astype(BF16)
    span = 2 * MAXSHIFT
    row = lax.broadcasted_iota(jnp.int32, (span, BLOCK), 0)
    above = (row_block > 0) | (row >= MAXSHIFT)
    below = (row_block < lax.axis_size("tm") - 1) | (row < MAXSHIFT)
    for at in range(0, width, BLOCK):
        psi, phi = (
            filter_rows(
                [ends.at[plane, i] for i in range(2 * epochs)],
                HALO - MAXSHIFT - RADIUS, span, at, lhs, corner_lhs, band_ref, corner_ref, plane,
            )
            for plane in range(2)
        )
        for i in range(2 * epochs):
            ep, inside = i % epochs, (above if i < epochs else below)
            values = weigh(psi[i], phi[i])
            for plane in range(2):
                slot = 2 * ep + plane
                turn = (span * slot) % rows
                held = jnp.where(inside, values[plane], 0.0)
                if i < epochs:
                    base = slot * LANES
                    turned[base + turn : base + turn + span, :] = held
                    inner = middle_ref[slot, :, at : at + BLOCK]
                    straight = rows - span - turn
                    if straight:
                        turned[base + turn + span : base + rows, :] = inner[:straight]
                    if turn:
                        turned[base : base + turn, :] = inner[straight:]
                else:
                    extra = 2 * epochs * LANES + slot * span
                    turned[extra : extra + span, :] = held
        for part in range(2 * epochs + 1):
            lanes = slice(part * LANES, (part + 1) * LANES)
            wide[MAXSHIFT + at : MAXSHIFT + at + BLOCK, lanes] = turned[lanes, :].T.astype(BF16)
    edge = jnp.zeros((MAXSHIFT, wide.shape[1]), BF16)
    wide[:MAXSHIFT] = edge
    wide[MAXSHIFT + width :] = edge
    cols = width // chips // 2
    for k in range(chips):
        start = jnp.bitwise_xor(chip, k) * (2 * cols)
        for third in range(3):
            rows_from = start + lax.rem(third + 2 * core, 3) * cols
            outs[k][third * cols : (third + 1) * cols] = wide[pl.ds(pl.multiple_of(rows_from, cols), cols), :]


def filter_border(main, odd, even, middle, bands, chips):
    _, epochs, rows, width = main.shape
    lanes = (2 * epochs + 1) * LANES
    span = 2 * MAXSHIFT
    piece = jax.ShapeDtypeStruct((width // chips + span, lanes), BF16)
    return pl.pallas_call(
        functools.partial(border_kernel, chips),
        out_shape=(piece,) * chips,
        in_specs=[VMEM] * (4 + len(bands)),
        out_specs=[VMEM] * chips,
        scratch_shapes=[
            pltpu.VMEM((2, 2 * epochs, 2 * HALO, width), BF16),
            pltpu.VMEM((2 * epochs * span, TAPS * BLOCK), BF16),
            pltpu.VMEM((2 * epochs * span, TAPS * LANES), BF16),
            pltpu.VMEM((lanes, BLOCK), F32),
            pltpu.VMEM((width + span, lanes), BF16),
        ],
        compiler_params=PARAMS,
        name="border",
    )(main, odd, even, middle, *bands)


def stack_kernel(slots, vels, first, final, shifts_ref, *refs):
    count = len(slots)
    scratch = 4 if final else 2
    pieces, refs, scratch = refs[:count], refs[count:-scratch], refs[-scratch:]
    frames, sems = scratch[:2]
    if not first:
        start_ref, refs = refs[0], refs[1:]
    place = lax.axis_index("space")
    chip, core = lax.div(place, 2), lax.rem(place, 2)
    cols = refs[-1].shape[-2]
    window = cols + 2 * MAXSHIFT
    parts = pieces[0].shape[1] // LANES
    epochs = (parts - 1) // 2
    for slot, (_, flip) in enumerate(slots):
        for half in range(2):
            own = 2 * cols * core if half == 0 else cols * (1 - core)
            start = pl.multiple_of(own, cols) if flip == 0 else half * cols
            for part in range(parts):
                base = (slot * parts + part) * window + half * cols
                frames[base : base + cols] = pieces[slot][
                    pl.ds(start, cols), part * LANES : (part + 1) * LANES
                ].astype(F32)
    total_epochs = shifts_ref.shape[0] // vels
    lane = lax.broadcasted_iota(jnp.int32, (cols, LANES), 1)

    def add_slot(slot, k, flip, v, upper, lower):
        owner = 2 * jnp.bitwise_xor(chip, k) + jnp.bitwise_xor(core, flip)
        for ep in range(epochs):
            epoch = owner * epochs + ep
            both = shifts_ref[pl.ds(v * total_epochs + epoch, 1), :][0, 0]
            right = lax.shift_right_logical(both, 6)
            down = jnp.bitwise_and(both, 63)
            base = slot * (parts * window) + right
            extra = frames[pl.ds(base + 2 * epochs * window, cols), :]
            sums = []
            for plane, total in ((0, upper), (1, lower)):
                part = 2 * ep + plane
                turn = 2 * MAXSHIFT * part
                spot = lane if turn == 0 else lax.rem(lane + (LANES - turn), LANES)
                held = frames[pl.ds(base + part * window, cols), :]
                merged = jnp.where(spot < down, extra, held)
                sums.append(total + pltpu.roll(merged, lax.rem(2 * LANES - turn - down, LANES), 1))
            upper, lower = sums
        return upper, lower

    def add_all(v):
        if first:
            sums = (jnp.zeros((cols, LANES), F32), jnp.zeros((cols, LANES), F32))
        else:
            sums = (start_ref[v, 0], start_ref[v, 1])
        for slot, (k, flip) in enumerate(slots):
            sums = add_slot(slot, k, flip, v, *sums)
        return sums

    unroll = vels if count <= 8 else 1
    if final:
        best_ref, score_ref = refs

        def visit(v, carry):
            top, total = carry
            upper, lower = add_all(v)
            like = upper * lax.rsqrt(jnp.maximum(lower, 0.02))
            return jnp.maximum(top, like), total + jnp.exp(like)

        top = jnp.full((cols, LANES), -jnp.inf, F32)
        top, total = lax.fori_loop(0, vels, visit, (top, jnp.zeros((cols, LANES), F32)), unroll=unroll)
        best, score = scratch[2:]
        best[...] = top
        best_copy = pltpu.make_async_copy(best, best_ref, sems.at[0])
        best_copy.start()
        score[...] = jnp.log(total / vels)
        score_copy = pltpu.make_async_copy(score, score_ref, sems.at[1])
        score_copy.start()
        best_copy.wait()
        score_copy.wait()
    else:
        (sum_ref,) = refs

        def keep(v, carry):
            sum_ref[v, 0], sum_ref[v, 1] = add_all(v)
            return carry

        lax.fori_loop(0, vels, keep, 0, unroll=unroll)


def stack_epochs(shifts, vels, slots, pieces, sums, final, cols, rows):
    parts = pieces[0].shape[1] // LANES
    if final:
        out_shape = (jax.ShapeDtypeStruct((cols, rows), F32),) * 2
    else:
        out_shape = (jax.ShapeDtypeStruct((vels, 2, cols, rows), F32),)
    scratch = [
        pltpu.VMEM((len(pieces) * parts * (cols + 2 * MAXSHIFT), LANES), F32),
        pltpu.SemaphoreType.DMA((2,)),
    ]
    if final:
        scratch += [pltpu.VMEM((cols, rows), F32)] * 2
    return pl.pallas_call(
        functools.partial(stack_kernel, slots, vels, not sums, final),
        out_shape=out_shape,
        in_specs=[VMEM] * (1 + len(pieces) + len(sums)),
        out_specs=[ANY if final else VMEM] * len(out_shape),
        scratch_shapes=scratch,
        compiler_params=PARAMS,
        name="stack_end" if final else "stack_part",
    )(shifts, *pieces, *sums)


def on_device(image, inv_var, psf, shifts):
    epochs, width, rows = image.shape
    devices = lax.axis_size("space")
    row_blocks = lax.axis_size("tm")
    chips = devices // 2
    table = jnp.sum((shifts + MAXSHIFT) * jnp.array([64, 1], jnp.int32), axis=2).reshape(-1, 1)

    main, even, odd, psf = prepare(image, inv_var, psf)
    evens = [(i, i + 1) for i in range(0, row_blocks - 1, 2)]
    odds = [(i, i + 1) for i in range(1, row_blocks - 1, 2)]
    even = lax.ppermute(even, "tm", evens + [(j, i) for i, j in evens])
    odd = lax.ppermute(odd, "tm", odds + [(j, i) for i, j in odds])
    bands = band_matrices(psf, width // BLOCK)
    middle = filter_middle(main, bands)
    sent = filter_border(main, odd, even, middle, bands, chips)

    swap = [(i, i ^ 1) for i in range(devices)]
    cols = width // devices

    got = {0: sent[0]}
    for k in range(1, chips):
        pairs = [(2 * i + c, 2 * (i ^ k) + c) for i in range(chips) for c in range(2)]
        got[k] = lax.ppermute(sent[k], "space", pairs)
    def stack(slots, sums, final):
        pieces = []
        for k, flip in slots:
            pieces.append(lax.ppermute(got[k][cols:], "space", swap) if flip else got[k])
        return stack_epochs(table, shifts.shape[0], slots, pieces, sums, final, cols, rows)

    last = chips // 2
    sums = stack([(k, flip) for k in reversed(range(chips)) if k != last for flip in range(2)], (), False)
    got[last], sums = lax.optimization_barrier((got[last], sums))
    sums = stack([(last, 0)], sums, False)
    return stack([(last, 1)], sums, True)


def solution(mesh):
    in_specs = (P("space", None, "tm"), P("space", None, "tm"), P(), P())
    out_specs = (P("space", "tm"), P("space", "tm"))
    return jax.shard_map(
        on_device, mesh=mesh, in_specs=in_specs, out_specs=out_specs, check_vma=False
    )
```
